32 devices in a mesh: dp: 4 (over y, core), section: 4 (over z), mp: 2 (over x).
Axes of the slice: x: 2, y: 2, z: 4, core: 2. Of those that a mesh axis runs over, the one named last changes fastest.
Arguments:
- features: bfloat16 [4, 16, 16, 1536], P('dp'), may hold values from -6 to 6
- spatial_kernel: float32 [49, 1536], replicated, may hold values from -0.875 to 0.875
- block_gain: float32 [1536], replicated, may hold values from 0.25 to 1.75
- expand_weight: bfloat16 [1536, 6144], P('dp', ('section', 'mp')), may hold values from -0.15625 to 0.15625
- reduce_weight: bfloat16 [6144, 1536], P(('section', 'mp'), 'dp'), may hold values from -0.078125 to 0.078125
- layer_scale: float32 [1536], replicated, may hold values from 0.25 to 1
- down_gain: float32 [1536], replicated, may hold values from 0.25 to 1.75
- down_weight: bfloat16 [6144, 3072], P('dp', ('section', 'mp')), may hold values from -0.078125 to 0.078125
- down_bias: float32 [3072], P(('section', 'mp')), may hold values from -3 to 3
- head_gain: float32 [3072], replicated, may hold values from 0.25 to 1.75
- head_proj: bfloat16 [3072, 1024], replicated, may hold values from -0.109375 to 0.109375
- text_embed: bfloat16 [4, 1024], P('dp'), may hold values from -6 to 6
Outputs:
- section_four: bfloat16 [4, 8, 8, 3072], P('dp', None, None, ('section', 'mp'))
- logits: float32 [4, 4], P('dp')
The draws below stay inside these ranges and needn't reach their ends.
All inputs are finite; a program needn't handle non-finite values.
Results may differ from the reference program's by a relative error of at most 0.013.
Values may be sent and summed in bfloat16 or wider, within the bound.
No kernel may reach another device: no remote copies, remote signals or barrier semaphores. Data moves between devices by JAX's collectives and lax.ppermute only.
A program may use at most 64 MiB of HBM per device.

```python
import math
import jax
import jax.numpy as jnp
from jax import lax

C3 = 1536
FF3 = 6144
C4 = 3072
EMBED = 1024
SIDE = 16
KERNEL = 7
IMG_DEV = 1
IMAGES = 4
N_DP = 4
N_SECTION = 4
N_MP = 2


def level_of(own_key, extent, split, least, largest):
    loudness = 1.0
    for position, blocks in split:
        draws = jax.random.uniform(jax.random.fold_in(jax.random.fold_in(own_key, 6), position), (blocks,), jnp.float32, least / len(split), largest / len(split))
        loudness = loudness * jnp.repeat(jnp.exp(draws), extent[position] // blocks).reshape((-1,) + (1,) * (len(extent) - 1 - position))
    return loudness


def noise(key, extent, deviation, most, split=(), kind=jnp.bfloat16):
    factor_of = level_of(key, extent, split, -0.22, 0.18) if split else 1.0
    drawn = jax.random.normal(key, extent, jnp.float32) * deviation * factor_of
    return jnp.minimum(jnp.maximum(drawn, -most), most).astype(kind)


def setup_inputs(seed: int = 0) -> dict:
    key_list = jax.random.split(jax.random.key(seed), 13)
    features = noise(key_list[0], (IMAGES, SIDE, SIDE, C3), 1.0, 6.0, ((0, 4),))
    spatial_kernel = noise(key_list[1], (KERNEL * KERNEL, C3), (KERNEL * KERNEL) ** -0.5, 0.875, (), jnp.float32)
    block_gain = jnp.clip(1.0 + 0.15 * jax.random.normal(key_list[2], (C3,), jnp.float32), 0.25, 1.75)
    expand_weight = noise(key_list[3], (C3, FF3), C3 ** -0.5, 0.15625, ((0, 4), (1, 8)))
    reduce_weight = noise(key_list[4], (FF3, C3), FF3 ** -0.5, 0.078125, ((0, 8), (1, 4)))
    layer_scale = jnp.clip(jnp.exp(jax.random.uniform(key_list[5], (C3,), jnp.float32, math.log(0.25), math.log(1.0))), 0.25, 1.0)
    down_gain = jnp.clip(1.0 + 0.15 * jax.random.normal(key_list[6], (C3,), jnp.float32), 0.25, 1.75)
    down_weight = noise(key_list[7], (4 * C3, C4), (4 * C3) ** -0.5, 0.078125, ((0, 4), (1, 8)))
    down_bias = noise(key_list[8], (C4,), 0.5, 3.0, ((0, 8),), jnp.float32)
    head_gain = jnp.clip(1.0 + 0.15 * jax.random.normal(key_list[9], (C4,), jnp.float32), 0.25, 1.75)
    head_proj = noise(key_list[10], (C4, EMBED), C4 ** -0.5, 0.109375)
    text_embed = noise(key_list[11], (IMAGES, EMBED), 1.0, 6.0, ((0, 4),))
    return dict(features=features, spatial_kernel=spatial_kernel, block_gain=block_gain, expand_weight=expand_weight, reduce_weight=reduce_weight, layer_scale=layer_scale, down_gain=down_gain, down_weight=down_weight, down_bias=down_bias, head_gain=head_gain, head_proj=head_proj, text_embed=text_embed)


def normalize(values, gain):
    center = values - lax.optimization_barrier(jnp.mean(values, axis=-1, keepdims=True))
    spread = lax.optimization_barrier(jnp.mean(center * center, axis=-1, keepdims=True))
    return center * lax.rsqrt(spread + 1e-06) * gain

def encode(group, spatial_kernel, block_gain, expand_weight, reduce_weight, layer_scale, down_gain, down_weight, down_bias, head_gain, head_proj):
    count = group.shape[0]
    pixel_rows = count * SIDE * SIDE
    padded = jnp.pad(group.astype(jnp.float32), ((0, 0), (3, 3), (3, 3), (0, 0)))
    spatial = jnp.zeros((count, SIDE, SIDE, C3), jnp.float32)
    for tap_row in range(KERNEL):
        for tap_col in range(KERNEL):
            spatial = spatial + padded[:, tap_row:tap_row + SIDE, tap_col:tap_col + SIDE, :] * spatial_kernel[tap_row * KERNEL + tap_col]
    normed = normalize(spatial, block_gain).astype(jnp.bfloat16).reshape(pixel_rows, C3)
    hidden = jax.nn.gelu(jnp.dot(normed, expand_weight, preferred_element_type=jnp.float32), approximate=False).astype(jnp.bfloat16)
    groups = N_SECTION * N_MP
    width = FF3 // groups
    partials = jnp.einsum('rgk,gkc->grc', hidden.reshape(pixel_rows, groups, width).astype(jnp.float32), reduce_weight.reshape(groups, width, C3).astype(jnp.float32))
    rounded = lax.optimization_barrier(partials.astype(jnp.bfloat16))
    branch = lax.optimization_barrier(jnp.sum(rounded.astype(jnp.float32), axis=0))
    resid = (group.reshape(pixel_rows, C3).astype(jnp.float32) + layer_scale * branch).astype(jnp.bfloat16)
    normed_two = normalize(resid.astype(jnp.float32), down_gain).astype(jnp.bfloat16)
    half = SIDE // 2
    patches = normed_two.reshape(count, half, 2, half, 2, C3).transpose(0, 1, 3, 2, 4, 5).reshape(count * half * half, 4 * C3)
    section_four = (jnp.dot(patches, down_weight, preferred_element_type=jnp.float32) + down_bias).astype(jnp.bfloat16)
    pooled = lax.optimization_barrier(jnp.mean(section_four.astype(jnp.float32).reshape(count, half * half, C4), axis=1))
    head = normalize(pooled, head_gain).astype(jnp.bfloat16)
    image = jnp.dot(head, head_proj, preferred_element_type=jnp.float32)
    image = image * lax.rsqrt(lax.optimization_barrier(jnp.sum(image * image, axis=-1, keepdims=True)) + 1e-06)
    return (section_four.reshape(count, half, half, C4), image)

def reference(features, spatial_kernel, block_gain, expand_weight, reduce_weight, layer_scale, down_gain, down_weight, down_bias, head_gain, head_proj, text_embed):
    blocks = features.reshape(N_DP, IMG_DEV, SIDE, SIDE, C3)

    def one_block(group):
        return encode(group, spatial_kernel, block_gain, expand_weight, reduce_weight, layer_scale, down_gain, down_weight, down_bias, head_gain, head_proj)
    section_four, image = lax.map(one_block, blocks)
    section_four = section_four.reshape(IMAGES, SIDE // 2, SIDE // 2, C4)
    image = image.reshape(IMAGES, EMBED)
    text = text_embed.astype(jnp.float32)
    text = text * lax.rsqrt(lax.optimization_barrier(jnp.sum(text * text, axis=-1, keepdims=True)) + 1e-06)
    logits = 100.0 * jnp.dot(image, text.T, precision=lax.Precision.HIGHEST, preferred_element_type=jnp.float32)
    return (section_four, logits)
```

```python
import functools
import jax
import jax.numpy as jnp
from jax import lax
from jax.experimental import pallas as pl
from jax.experimental.pallas import tpu as pltpu
from jax.sharding import PartitionSpec as P

EPS = 1e-06
TAPS = 4
UNITS = ("section", "mp")

VMEM = pl.BlockSpec(memory_space=pltpu.VMEM)
SMEM = pl.BlockSpec(memory_space=pltpu.SMEM)


def call(body, out_shape, n_smem, n_vmem, name):
    many = isinstance(out_shape, (tuple, list))
    return pl.pallas_call(
        body,
        out_shape=out_shape,
        in_specs=[SMEM] * n_smem + [VMEM] * n_vmem,
        out_specs=[VMEM] * len(out_shape) if many else VMEM,
        name=name,
    )


def normalize(values, gain):
    center = values - jnp.mean(values, axis=-1, keepdims=True)
    spread = jnp.mean(center * center, axis=-1, keepdims=True)
    return center * lax.rsqrt(spread + EPS) * gain


def pieces_over(value, axis, n, dim):
    me = lax.axis_index(axis)
    if n & (n - 1) or n > TAPS:
        return [lax.all_gather(value, axis, axis=dim, tiled=True)], jnp.zeros((1,), jnp.int32)
    held = [(0, value)]
    step = n // 2
    while step:
        swap = [(i, i ^ step) for i in range(n)]
        held += [(k ^ step, lax.ppermute(v, axis, swap)) for k, v in held]
        step //= 2
    offsets = jnp.array([k for k, _ in held], jnp.int32)
    return [v for _, v in held], jnp.bitwise_xor(me.astype(jnp.int32), offsets)


def expand_body(parts, block_ref, normed_ref, *refs):
    out_ref = refs[-1]
    total = None
    for j in range(parts):
        part = jnp.dot(normed_ref[block_ref[j]], refs[j][...], preferred_element_type=jnp.float32)
        total = part if total is None else total + part
    out_ref[...] = (0.5 * total * (1.0 + lax.erf(total * (0.5**0.5)))).astype(out_ref.dtype)


def reduce_body(parts, block_ref, hidden_ref, *refs):
    out_ref = refs[-1]
    width = refs[0].shape[1]
    for j in range(parts):
        part = jnp.dot(hidden_ref[...], refs[j][...], preferred_element_type=jnp.float32)
        start = pl.multiple_of(block_ref[j] * width, 128)
        out_ref[:, pl.ds(start, width)] = part.astype(out_ref.dtype)


def resid_body(parts_ref, feat_ref, scale_ref, gain_ref, out_ref):
    branch = jnp.sum(parts_ref[...].astype(jnp.float32), axis=0)
    resid = (feat_ref[...].astype(jnp.float32) + scale_ref[...] * branch).astype(jnp.bfloat16)
    out_ref[...] = normalize(resid.astype(jnp.float32), gain_ref[...]).astype(out_ref.dtype)


def split3(value):
    high = value.astype(jnp.bfloat16)
    rest = value - high.astype(jnp.float32)
    mid = rest.astype(jnp.bfloat16)
    low = (rest - mid.astype(jnp.float32)).astype(jnp.bfloat16)
    return high, mid, low


def down_body(parts, merged, block_ref, acts_ref, bias_ref, gain_ref, proj_ref, *refs):
    out_ref, note_ref = refs[-2], refs[-1]
    rows = out_ref.shape[0]
    per = TAPS // parts
    depth = refs[0].shape[0] // per
    total = None
    for j in range(parts):
        for u in range(per):
            tap = block_ref[j] * per + u
            if merged:
                acts = acts_ref[tap]
            else:
                acts = acts_ref[:, tap].astype(jnp.float32).reshape(rows, depth).astype(jnp.bfloat16)
            part = jnp.dot(acts, refs[j][u * depth : (u + 1) * depth], preferred_element_type=jnp.float32)
            total = part if total is None else total + part
    four = (total + bias_ref[...]).astype(jnp.bfloat16)
    out_ref[...] = four
    pooled = jnp.mean(four.astype(jnp.float32), axis=0, keepdims=True)
    middle = jnp.mean(pooled, axis=-1, keepdims=True)
    center = pooled - middle
    spread = jnp.sum(center * center, axis=-1, keepdims=True)
    gain = gain_ref[...]
    stack = jnp.concatenate(
        [s.astype(jnp.float32) for s in split3(center * gain) + split3(gain)]
        + [jnp.zeros((2, gain.shape[1]), jnp.float32)],
        axis=0,
    ).astype(jnp.bfloat16)
    both = jnp.dot(stack, proj_ref[...], preferred_element_type=jnp.float32)
    width = both.shape[1]
    note_ref[0:1, 0:width] = both[0:1] + both[1:2] + both[2:3]
    note_ref[0:1, width : 2 * width] = both[3:4] + both[4:5] + both[5:6]
    lane = lax.broadcasted_iota(jnp.int32, (1, 128), 1)
    note_ref[0:1, 2 * width :] = jnp.where(lane == 0, middle, jnp.where(lane == 1, spread, 0.0))


def head_body(share, notes_ref, text_ref, out_ref):
    units = notes_ref.shape[0]
    width = text_ref.shape[1]
    notes = notes_ref[...]
    stats = notes[:, 2 * width :]
    middles, spreads = stats[:, 0:1], stats[:, 1:2]
    delta = middles - jnp.mean(middles, axis=0, keepdims=True)
    spread = jnp.sum(spreads + share * delta * delta, axis=0, keepdims=True) / (share * units)
    raw = jnp.sum(notes[:, :width] + delta * notes[:, width : 2 * width], axis=0, keepdims=True)
    image = raw * lax.rsqrt(spread + EPS)
    image = image * lax.rsqrt(jnp.sum(image * image, axis=-1, keepdims=True) + EPS)
    text = text_ref[...].astype(jnp.float32)
    text = text * lax.rsqrt(jnp.sum(text * text, axis=-1, keepdims=True) + EPS)
    out_ref[...] = 100.0 * jnp.sum(image * text, axis=-1, keepdims=True)


def per_device(
    sizes,
    features,
    spatial_kernel,
    block_gain,
    expand_weight,
    reduce_weight,
    layer_scale,
    down_gain,
    down_weight,
    down_bias,
    head_gain,
    head_proj,
    text_embed,
):
    count, side, _, channels = features.shape
    pixels = side * side
    n_dp = sizes["dp"]
    units = sizes["section"] * sizes["mp"]
    unit = lax.axis_index(UNITS)
    half = side // 2
    chunk = pixels // units
    patches = chunk // TAPS

    ups, blocks = pieces_over(expand_weight, "dp", n_dp, 0)
    backs, _ = pieces_over(reduce_weight, "dp", n_dp, 1)
    downs, _ = pieces_over(down_weight, "dp", n_dp, 0)
    parts = len(ups)

    def by_patch(maps):
        maps = maps.reshape(half, 2, half, 2, channels).transpose(0, 2, 1, 3, 4)
        maps = maps.reshape(units, patches, TAPS, channels).transpose(0, 2, 1, 3)
        return maps.reshape(units, chunk, channels)

    padded = jnp.pad(features.astype(jnp.float32), ((0, 0), (3, 3), (3, 3), (0, 0)))
    spatial = jnp.zeros(features.shape, jnp.float32)
    for row in range(7):
        for col in range(7):
            spatial = (
                spatial + padded[:, row : row + side, col : col + side, :] * spatial_kernel[row * 7 + col]
            )
    normed = by_patch(normalize(spatial, block_gain).astype(jnp.bfloat16))
    normed = normed.reshape(pixels, parts, channels // parts).transpose(1, 0, 2)
    feat = lax.dynamic_index_in_dim(by_patch(features), unit, 0, keepdims=False)

    hidden_width = expand_weight.shape[1]
    hidden = call(
        functools.partial(expand_body, parts),
        jax.ShapeDtypeStruct((pixels, hidden_width), jnp.bfloat16),
        1,
        1 + parts,
        "expand",
    )(blocks, normed, *ups)
    branch = call(
        functools.partial(reduce_body, parts),
        jax.ShapeDtypeStruct((pixels, channels), jnp.bfloat16),
        1,
        1 + parts,
        "reduce",
    )(blocks, hidden, *backs)
    shares = lax.all_to_all(branch.reshape(units, chunk, channels), UNITS, 0, 0, tiled=True)
    mine = call(
        resid_body,
        jax.ShapeDtypeStruct((chunk, channels), jnp.bfloat16),
        0,
        4,
        "resid",
    )(shares, feat, layer_scale[None], down_gain[None])
    acts = lax.all_to_all(
        jnp.broadcast_to(mine[None], (units, chunk, channels)), UNITS, 0, 0, tiled=True
    )
    acts = acts.reshape(units, TAPS, patches, channels)
    merged = patches % 8 != 0
    if merged:
        acts = acts.transpose(1, 0, 2, 3).reshape(TAPS, units * patches, channels)

    out_width = down_weight.shape[1]
    embed = head_proj.shape[1]
    gain_row = lax.dynamic_slice_in_dim(head_gain, unit * out_width, out_width)[None]
    proj = lax.dynamic_slice_in_dim(head_proj, unit * out_width, out_width)
    four, note = call(
        functools.partial(down_body, parts, merged),
        (
            jax.ShapeDtypeStruct((half * half, out_width), jnp.bfloat16),
            jax.ShapeDtypeStruct((1, 2 * embed + 128), jnp.float32),
        ),
        1,
        4 + parts,
        "down",
    )(blocks, acts, down_bias[None], gain_row, proj, *downs)
    notes = lax.all_to_all(
        jnp.broadcast_to(note[None], (units,) + note.shape), UNITS, 0, 0, tiled=True
    ).reshape(units, note.shape[1])
    texts, text_blocks = pieces_over(text_embed, "dp", n_dp, 0)
    text = jnp.concatenate(texts, axis=0)
    logits = call(
        functools.partial(head_body, out_width),
        jax.ShapeDtypeStruct((text.shape[0], 1), jnp.float32),
        0,
        2,
        "head",
    )(notes, text)[:, 0]
    if len(texts) > 1:
        logits = jnp.zeros_like(logits).at[text_blocks].set(logits)
    return (four.reshape(count, half, half, out_width), logits[None])


def solution(mesh):
    placed = (
        P("dp", None, None, None),
        P(),
        P(),
        P("dp", UNITS),
        P(UNITS, "dp"),
        P(),
        P(),
        P("dp", UNITS),
        P(UNITS),
        P(),
        P(),
        P("dp", None),
    )
    return jax.shard_map(
        functools.partial(per_device, dict(mesh.shape)),
        mesh=mesh,
        in_specs=placed,
        out_specs=(P("dp", None, None, UNITS), P("dp", None)),
        check_vma=False,
    )
```
